1024 devices in a mesh: dp: 128 (over x, y, core), group: 8 (over z).
Axes of the slice: x: 8, y: 8, z: 8, core: 2. Of those that a mesh axis runs over, the one named last changes fastest.
Arguments:
- features: bfloat16 [128, 8, 256, 1536], P('dp', 'group'), may hold values from -6 to 6
- cotangent: bfloat16 [128, 8, 256, 1536], P('dp', 'group'), may hold values from -24 to 24
- lengths: int32 [128, 8, 4], P('dp', 'group'), may hold values from 1 to 128, 256 in all within a row
- destination: int32 [128, 8, 2], P('dp', 'group'), may hold values from 0 to 1, as said below
- kernel: float32 [31, 1536], replicated, may hold values from -1 to 1
- norm_gain: float32 [1536], replicated, may hold values from 0.1 to 1.9
- norm_bias: float32 [1536], replicated, may hold values from -3 to 3
Outputs:
- input_grad: bfloat16 [128, 8, 256, 1536], P('dp', 'group')
- kernel_grad: float32 [31, 1536], P(None, 'dp')
- norm_grad: float32 [2, 1536], P(None, 'dp')
The draws below stay inside these ranges and needn't reach their ends.
Inputs may be any that keep to these rules, and one draw needn't show every extreme that they name: Each device's lengths sum to 256, and the longest is exactly half of 256. `destination`: exactly 1 of each device's 2 blocks are marked 1.
All inputs are finite; a program needn't handle non-finite values.
Results may differ from the reference program's by a relative error of at most 0.001.
Values may be sent and summed in bfloat16 or wider, within the bound.
A program may use at most 32 MiB of HBM per device.

```python
import math
import jax
import jax.numpy as jnp
import numpy as np
from jax import lax

C = 1536
KW = 31
BLK = 128
MOVE = 1
FR_DEV = 256
UTT = 4
NB = 2
N_DP = 128
N_GROUP = 8


def draw_destination(key, part):
    scores = jax.random.randint(key, (N_DP, N_GROUP, NB), 0, 1 << 20) * NB + jnp.arange(NB, dtype=jnp.int32)
    ranking = jnp.argsort(jnp.argsort(scores, axis=-1), axis=-1)
    return (ranking < MOVE).astype(jnp.int32)


def strengthened(drawn, stream_key, source, target, parts, factor):
    def block_of(dim):
        return (jnp.arange(drawn.shape[dim]) // (drawn.shape[dim] // parts)).reshape((-1,) + (1,) * (drawn.ndim - 1 - dim))

    one_side = jax.random.permutation(stream_key, parts)[block_of(target)]
    other_side = (block_of(target) + parts // 2) % parts
    return jnp.where((block_of(source) == one_side) | (block_of(source) == other_side), factor * drawn, drawn)


def levels(own_key, extent, pieces, smallest, largest):
    loudness = 1.0
    for axis_at, parts in pieces:
        heights = jax.random.uniform(jax.random.fold_in(jax.random.fold_in(own_key, 6), axis_at), (parts,), jnp.float32, smallest / len(pieces), largest / len(pieces))
        loudness = loudness * jnp.repeat(jnp.exp(heights), extent[axis_at] // parts).reshape((-1,) + (1,) * (len(extent) - 1 - axis_at))
    return loudness


def length_profile(amount, total, reach, skew):
    portions = [(1 << 20) // math.isqrt(rank ** skew) + 1 for rank in range(2, amount + 1)]
    spare, counts = total - reach - (amount - 1), [1] * (amount - 1)
    while spare > 0:
        free = [i for i in range(amount - 1) if counts[i] < reach]
        pool, remaining = sum([portions[i] for i in free]), spare
        for i in free:
            more = min(reach - counts[i], max(1, remaining * portions[i] // pool), spare)
            counts[i] = counts[i] + more
            spare = spare - more
    return np.array([reach] + counts)


def uneven_parts(rng, amount, total, reach, slope):
    if amount == 2:
        one = jax.random.randint(rng, (), max(1, total - reach), min(reach, total - 1) + 1)
        return jnp.stack([one, total - one])
    sizes = jnp.asarray(length_profile(amount, total, reach, slope), jnp.int32)
    pairs = (amount - 1) // 2
    source_of, sink = sizes[1:1 + 2 * pairs:2], sizes[2:2 + 2 * pairs:2]
    room = jnp.minimum(source_of - 1, reach - sink)
    moved = jax.random.randint(jax.random.fold_in(rng, 1), (pairs,), 0, 1 << 20) % (room + 1)
    sizes = sizes.at[1:1 + 2 * pairs:2].set(source_of - moved).at[2:2 + 2 * pairs:2].set(sink + moved)
    return sizes[jax.random.permutation(jax.random.fold_in(rng, 2), amount)]


def bell_draw(key, dims, scale, reach, pieces=(), held_as=jnp.bfloat16):
    drawn = jax.random.normal(key, dims, jnp.float32) * scale
    if len(pieces) > 0:
        drawn = levels(key, dims, pieces, -0.22, 0.18) * drawn
    return jnp.clip(drawn, min=-reach, max=reach).astype(held_as)


def noise_with(key, dims, deviation, bound, split, heavy, kind=jnp.bfloat16):
    entries = deviation * jax.random.normal(key, dims, jnp.float32)
    if split:
        entries = entries * levels(key, dims, split, -0.22, 0.18)
    return jnp.clip(strengthened(entries, jax.random.fold_in(key, 3), *heavy), -bound, bound).astype(kind)


def setup_inputs(seed: int = 0) -> dict:
    seeds = jax.random.split(jax.random.key(seed), 8)
    return {
        "features": bell_draw(seeds[0], (N_DP, N_GROUP, FR_DEV, C), 1.0, 6.0, ((0, 128), (1, 8))),
        "cotangent": noise_with(seeds[1], (N_DP, N_GROUP, FR_DEV, C), 1.0, 24.0, ((0, 128), (1, 8)), (0, 3, 128, 5.5)),
        "lengths": jax.vmap(lambda own: uneven_parts(own, UTT, FR_DEV, FR_DEV // 2, 2))(jax.random.split(seeds[2], N_DP * N_GROUP)).reshape((N_DP, N_GROUP, UTT)).astype(jnp.int32),
        "destination": draw_destination(jax.random.fold_in(seeds[7], 71), 0),
        "kernel": bell_draw(seeds[4], (KW, C), KW ** -0.5, 1.0, (), jnp.float32),
        "norm_gain": jnp.clip(1.0 + 0.18 * jax.random.normal(seeds[5], (C,), jnp.float32), 0.1, 1.9),
        "norm_bias": bell_draw(seeds[6], (C,), 0.5, 3.0, (), jnp.float32),
    }


EPSILON = 1e-05

def local_pass(features, cotangent, lengths, kernel, norm_gain, norm_bias):
    frames = features.shape[0]
    tap_count = kernel.shape[0]
    half_span = tap_count // 2
    utt_ends = jnp.cumsum(lengths).astype(jnp.int32)
    starts = (utt_ends - lengths).astype(jnp.int32)
    position = jnp.arange(frames, dtype=jnp.int32)
    inside = (position[:, None] >= starts[None, :]) & (position[:, None] < utt_ends[None, :])
    utt_start = lax.optimization_barrier(jnp.sum(jnp.where(inside, starts[None, :], 0), axis=1))
    utt_end = lax.optimization_barrier(jnp.sum(jnp.where(inside, utt_ends[None, :], 0), axis=1))
    source = features.astype(jnp.float32)
    padded = jnp.pad(source, ((half_span, half_span), (0, 0)))
    inside_masks = []
    mixed_conv = jnp.zeros_like(source)
    for tap_index in range(tap_count):
        target = position + (tap_index - half_span)
        inside_mask = ((target >= utt_start) & (target < utt_end)).astype(jnp.float32)[:, None]
        inside_masks.append(inside_mask)
        mixed_conv = mixed_conv + kernel[tap_index] * padded[tap_index:tap_index + frames] * inside_mask
    row_mean = lax.optimization_barrier(jnp.mean(mixed_conv, axis=1, keepdims=True))
    centred = mixed_conv - row_mean
    variance = lax.optimization_barrier(jnp.mean(centred * centred, axis=1, keepdims=True))
    inv_scale = lax.rsqrt(variance + EPSILON)
    normed = centred * inv_scale
    activation = normed * norm_gain + norm_bias
    sigmoid_act = jax.nn.sigmoid(activation)
    dact = cotangent.astype(jnp.float32) * sigmoid_act * (1.0 + activation * (1.0 - sigmoid_act))
    gain_term = lax.optimization_barrier(jnp.sum(dact * normed, axis=0))
    bias_term = lax.optimization_barrier(jnp.sum(dact, axis=0))
    dnorm = dact * norm_gain
    dconv = inv_scale * (dnorm - lax.optimization_barrier(jnp.mean(dnorm, axis=1, keepdims=True)) - normed * lax.optimization_barrier(jnp.mean(dnorm * normed, axis=1, keepdims=True)))
    kernel_rows = []
    input_terms = jnp.zeros_like(source)
    for tap_index in range(tap_count):
        weighted = dconv * inside_masks[tap_index]
        kernel_rows.append(lax.optimization_barrier(jnp.sum(weighted * padded[tap_index:tap_index + frames], axis=0)))
        shifted = jnp.pad(weighted, ((half_span, half_span), (0, 0)))
        begin = 2 * half_span - tap_index
        input_terms = input_terms + kernel[tap_index] * shifted[begin:begin + frames]
    kernel_term = jnp.stack(kernel_rows, axis=0)
    norm_term = jnp.stack([gain_term, bias_term], axis=0)
    return (input_terms.astype(jnp.bfloat16), kernel_term, norm_term)

def reference(features, cotangent, lengths, destination, kernel, norm_gain, norm_bias):
    channels = features.shape[3]
    device_count = N_DP * N_GROUP
    flat_feat = features.reshape(device_count, FR_DEV, channels)
    flat_cot = cotangent.reshape(device_count, FR_DEV, channels)
    flat_len = lengths.reshape(device_count, UTT)

    def one_device(running, device_items):
        local_grad, kernel_term, norm_term = local_pass(device_items[0], device_items[1], device_items[2], kernel, norm_gain, norm_bias)
        return ((running[0] + kernel_term, running[1] + norm_term), local_grad)
    start_sums = (jnp.zeros((KW, channels), jnp.float32), jnp.zeros((2, channels), jnp.float32))
    sums_out, local_grads = lax.scan(one_device, start_sums, (flat_feat, flat_cot, flat_len))
    grad_scale = 1.0 / jnp.sqrt(jnp.float32(device_count * FR_DEV))
    kernel_grad = sums_out[0] * grad_scale
    norm_grad = sums_out[1] * grad_scale
    blocks = local_grads.reshape(N_DP, N_GROUP, NB, BLK, channels)
    block_order = jnp.argsort(destination * NB + jnp.arange(NB, dtype=jnp.int32), axis=-1).astype(jnp.int32)
    sorted_blocks = jnp.take_along_axis(blocks, block_order[:, :, :, None, None], axis=2)
    staying = sorted_blocks[:, :, :NB - MOVE]
    movers = jnp.roll(sorted_blocks[:, :, NB - MOVE:], 1, axis=0)
    input_grad = jnp.concatenate([staying, movers], axis=2).reshape(N_DP, N_GROUP, FR_DEV, channels)
    return (input_grad, kernel_grad, norm_grad)
```

```python
import math

import jax
import jax.numpy as jnp
from jax import lax
from jax.experimental import pallas as pl
from jax.experimental.pallas import tpu as pltpu
from jax.sharding import PartitionSpec as P

EPSILON = 1e-05
GAP = 16
LANES = 128
KEEP = 40
TILE = 8
CORES = 2
MESH = pl.DeviceIdType.MESH


def tap_groups(taps):
    return [[k for k in range(phase, taps, TILE)] for phase in range(TILE)]


def convolve(source, row, weights, taps, rows):
    total = None
    for group in tap_groups(taps):
        window = source[pl.ds(row + group[0], rows + TILE * (len(group) - 1)), :]
        for step, tap in enumerate(group):
            term = weights(tap) * window[TILE * step : TILE * step + rows]
            total = term if total is None else total + term
    return total


def local_kernel(
    lengths, destination, features, cotangent, kernel, gain, bias,
    grad_out, packed_out,
    stage, padded, conv, dnorm, dconv, owner, row_a, row_b, mean, scale, tap_sums, terms, columnwise,
):
    frames, channels = features.shape
    utterances = lengths.shape[0]
    taps = kernel.shape[0]
    half_span = taps // 2
    blocks = channels // LANES
    spread = frames + GAP * (utterances - 1)
    margin = GAP * (utterances - 1)
    chunk = spread // 2
    inverse = 1.0 / channels

    place = lax.broadcasted_iota(jnp.int32, (spread, LANES), 0)
    wide_owner = jnp.full((spread, LANES), -1, jnp.int32)
    begin = 0
    for u in range(utterances):
        finish = begin + lengths[u]
        here = (place >= begin + GAP * u) & (place < finish + GAP * u)
        wide_owner = jnp.where(here, u, wide_owner)
        begin = finish
    owner[...] = wide_owner

    edge = jnp.zeros((GAP, LANES), jnp.float32)
    terms[...] = jnp.zeros_like(terms)

    def spread_rows(value):
        stage[pl.ds(margin, frames), :] = value
        ids = owner[...]
        out = jnp.zeros((spread, LANES), jnp.float32)
        for u in range(utterances):
            out = jnp.where(ids == u, stage[pl.ds(margin - GAP * u, spread), :], out)
        return out

    def columns(b):
        return pl.ds(pl.multiple_of(b * LANES, LANES), LANES)

    def row_total(ref):
        return jnp.broadcast_to(jnp.sum(ref[...], axis=1, keepdims=True), (spread, LANES))

    stage[...] = jnp.zeros_like(stage)
    row_a[...] = jnp.zeros_like(row_a)

    @pl.loop(0, blocks)
    def _(b):
        padded[b, pl.ds(0, GAP), :] = edge
        padded[b, pl.ds(GAP + spread, GAP), :] = edge
        padded[b, pl.ds(GAP, spread), :] = spread_rows(features[:, columns(b)].astype(jnp.float32))
        for c in range(2):
            value = convolve(
                padded.at[b], GAP - half_span + chunk * c,
                lambda tap: kernel[pl.ds(tap, 1), columns(b)], taps, chunk,
            )
            conv[b, pl.ds(chunk * c, chunk), :] = value
            row_a[pl.ds(chunk * c, chunk), :] += value

    mean[...] = row_total(row_a) * inverse
    row_a[...] = jnp.zeros_like(row_a)

    @pl.loop(0, blocks)
    def _(b):
        centred = conv[b] - mean[...]
        conv[b] = centred
        row_a[...] += centred * centred

    scale[...] = lax.rsqrt(row_total(row_a) * inverse + EPSILON)
    row_a[...] = jnp.zeros_like(row_a)
    row_b[...] = jnp.zeros_like(row_b)

    @pl.loop(0, blocks)
    def _(b):
        normed = conv[b] * scale[...]
        conv[b] = normed
        g = gain[:, columns(b)]
        act = normed * g + bias[:, columns(b)]
        gate = jax.nn.sigmoid(act)
        dact = spread_rows(cotangent[:, columns(b)].astype(jnp.float32)) * gate * (1.0 + act * (1.0 - gate))
        terms[pl.ds(taps, 1), columns(b)] = jnp.sum(dact * normed, axis=0, keepdims=True)
        terms[pl.ds(taps + 1, 1), columns(b)] = jnp.sum(dact, axis=0, keepdims=True)
        weighted = dact * g
        dnorm[b] = weighted
        row_a[...] += weighted
        row_b[...] += weighted * normed

    mean[...] = row_total(row_a) * inverse
    row_b[...] = row_total(row_b) * inverse

    @pl.loop(0, blocks)
    def _(b):
        dconv[b, pl.ds(0, GAP), :] = edge
        dconv[b, pl.ds(GAP + spread, GAP), :] = edge
        dconv[b, pl.ds(GAP, spread), :] = scale[...] * (dnorm[b] - mean[...] - conv[b] * row_b[...])
        for c in range(2):
            ours = dconv[b, pl.ds(GAP + chunk * c, chunk), :]
            for group in tap_groups(taps):
                window = padded[
                    b, pl.ds(GAP - half_span + chunk * c + group[0], chunk + TILE * (len(group) - 1)), :
                ]
                for step, tap in enumerate(group):
                    product = ours * window[TILE * step : TILE * step + chunk]
                    part = jnp.sum(product.reshape(chunk // TILE, TILE, LANES), axis=0)
                    tap_sums[tap] = part if c == 0 else tap_sums[tap] + part
        terms[pl.ds(0, taps), columns(b)] = jnp.sum(tap_sums[...], axis=1)
        square = jnp.concatenate([terms[:, columns(b)], jnp.zeros((LANES - KEEP, LANES), jnp.float32)], axis=0)
        columnwise[columns(b), :] = square.T

    halves, lines, share = packed_out.shape[:3]
    depth = channels // (halves * lines * share)

    @pl.loop(0, lines)
    def _(x):
        for y in range(halves * share):
            first = (x * halves * share + y) * depth
            tile = None
            for a in range(depth // TILE):
                piece = columnwise[pl.ds(pl.multiple_of(first + TILE * a, TILE), TILE), :]
                piece = piece if a == 0 else pltpu.roll(piece, KEEP * a, 1)
                tile = piece if tile is None else tile + piece
            packed_out[y // share, x, y % share] = tile

    @pl.loop(0, blocks)
    def _(b):
        for c in range(2):
            stage[pl.ds(chunk * c, chunk), :] = convolve(
                dconv.at[b], GAP - half_span + chunk * c,
                lambda tap: kernel[pl.ds(taps - 1 - tap, 1), columns(b)], taps, chunk,
            )
        spot = lax.broadcasted_iota(jnp.int32, (frames, LANES), 0)
        grad = stage[pl.ds(0, frames), :]
        begin = lengths[0]
        for u in range(1, utterances):
            grad = jnp.where(spot >= begin, stage[pl.ds(GAP * u, frames), :], grad)
            begin = begin + lengths[u]
        grad = grad.astype(grad_out.dtype)
        size = grad_out.shape[1]
        for i in range(frames // size):
            grad_out[destination[i], :, columns(b)] = grad[size * i : size * (i + 1)]


def local_pass(features, cotangent, lengths, destination, kernel, gain, bias, side=8):
    frames, channels = features.shape
    utterances = lengths.shape[0]
    taps = kernel.shape[0]
    size = frames // destination.shape[0]
    blocks = channels // LANES
    spread = frames + GAP * (utterances - 1)
    margin = GAP * (utterances - 1)
    smem = pl.BlockSpec(memory_space=pltpu.SMEM)
    vmem = pl.BlockSpec(memory_space=pltpu.VMEM)
    f32 = jnp.float32
    return pl.pallas_call(
        local_kernel,
        out_shape=(
            jax.ShapeDtypeStruct((2, size, channels), jnp.bfloat16),
            jax.ShapeDtypeStruct((CORES, side, side // CORES, TILE, LANES), f32),
        ),
        in_specs=[smem, smem] + [vmem] * 5,
        out_specs=[vmem, vmem],
        scratch_shapes=[
            pltpu.VMEM((margin + spread, LANES), f32),
            pltpu.VMEM((blocks, spread + 2 * GAP, LANES), f32),
            pltpu.VMEM((blocks, spread, LANES), f32),
            pltpu.VMEM((blocks, spread, LANES), f32),
            pltpu.VMEM((blocks, spread + 2 * GAP, LANES), f32),
            pltpu.VMEM((spread, LANES), jnp.int32),
            pltpu.VMEM((spread, LANES), f32),
            pltpu.VMEM((spread, LANES), f32),
            pltpu.VMEM((spread, LANES), f32),
            pltpu.VMEM((spread, LANES), f32),
            pltpu.VMEM((taps, TILE, LANES), f32),
            pltpu.VMEM((KEEP, channels), f32),
            pltpu.VMEM((channels, LANES), f32),
        ],
        name="conv_block",
    )(lengths, destination, features, cotangent, kernel, gain[None], bias[None])


def share_kernel(
    side, depth_z, divisor,
    grads, packed,
    grad_out, kernel_out, norm_out,
    from_core, sum_core, from_x, sum_x, from_y, sum_y, from_z,
    core_sent, core_got, x_sent, x_got, y_sent, y_got, z_sent, z_got, move_sent, move_got, stay_done,
):
    me = lax.axis_index("dp")
    z = lax.axis_index("group")
    ring = side * side * CORES
    core = lax.rem(me, CORES)
    chip = lax.div(me, CORES)
    y = lax.rem(chip, side)
    x = lax.div(chip, side)
    share = side // CORES

    def at(x, y, core):
        return ((x * side + y) * CORES + core, z)

    partner = at(x, y, 1 - core)
    following = (lax.rem(me + 1, ring), z)
    beside = (lax.rem(me + ring + 2 * core - 1, ring), z)
    x_steps = sorted(range(1, side), key=lambda d: -min(d, side - d))
    z_steps = sorted(range(1, depth_z), key=lambda d: -min(d, depth_z - d))

    def x_at(step):
        return lax.rem(x + step, side)

    def z_at(step):
        return lax.rem(z + step, depth_z)

    barrier = pltpu.get_barrier_semaphore()
    peers = [partner, beside]
    peers += [at(x_at(d), y, core) for d in range(1, side)]
    peers += [at(x, lax.rem(y + d, side), c) for d in range(1, side) for c in range(CORES)]
    peers += [(me, z_at(d)) for d in range(1, depth_z)]
    for peer in peers:
        pl.semaphore_signal(barrier, inc=1, device_id=peer, device_id_type=MESH)
    pl.semaphore_wait(barrier, len(peers))

    def remote(source, target, sent, got, device):
        return pltpu.make_async_remote_copy(
            src_ref=source, dst_ref=target, send_sem=sent, recv_sem=got, device_id=device, device_id_type=MESH
        )

    size = grads.shape[1]
    core_copies = []
    for d in x_steps + [0]:
        row = x_at(d)
        copy = remote(packed.at[1 - core, row], from_core.at[row], core_sent.at[row], core_got.at[row], partner)
        copy.start()
        core_copies.append(copy)
    move = remote(grads.at[1], grad_out.at[pl.ds(size, size)], move_sent, move_got, following)
    move.start()
    stay = pltpu.make_async_copy(grads.at[0], grad_out.at[pl.ds(0, size)], stay_done)
    stay.start()

    x_copies = []
    for d in x_steps:
        row = x_at(d)
        remote(packed.at[1 - core, row], from_core.at[row], core_sent.at[row], core_got.at[row], partner).wait_recv()
        sum_core[row] = packed[core, row] + from_core[row]
        copy = remote(sum_core.at[row], from_x.at[d - 1], x_sent.at[d - 1], x_got.at[d - 1], at(row, y, core))
        copy.start()
        x_copies.append(copy)
    remote(packed.at[1 - core, x], from_core.at[x], core_sent.at[x], core_got.at[x], partner).wait_recv()
    total = packed[core, x] + from_core[x]
    for d in reversed(x_steps):
        remote(sum_core.at[x], from_x.at[d - 1], x_sent.at[d - 1], x_got.at[d - 1], at(x, y, core)).wait_recv()
        total = total + from_x[d - 1]
    sum_x[...] = total

    holder = lax.div(y, share)
    y_copies = []
    for j in range(share):
        for c in range(CORES):
            goal = share * core + j
            away = jnp.logical_or(goal != y, core != c)
            copy = remote(
                sum_x.at[j], from_y.at[y], y_sent.at[j * CORES + c], y_got.at[y], at(x, goal, c)
            )
            pl.when(away)(copy.start)
            y_copies.append((away, copy))

    @pl.when(holder == core)
    def _():
        from_y[y] = sum_x[lax.rem(y, share)]

    for s in range(side):
        arrives = jnp.logical_or(s != y, holder != core)
        waiter = remote(sum_x.at[0], from_y.at[s], y_sent.at[0], y_got.at[s], at(x, s, holder))
        pl.when(arrives)(waiter.wait_recv)
    total = from_y[0]
    for s in range(1, side):
        total = total + from_y[s]
    sum_y[...] = total
    z_copies = []
    for d in z_steps:
        copy = remote(sum_y, from_z.at[z], z_sent.at[d - 1], z_got.at[z], (me, z_at(d)))
        copy.start()
        z_copies.append(copy)
    from_z[z] = total
    for d in z_steps:
        source = z_at(d)
        remote(sum_y, from_z.at[source], z_sent.at[d - 1], z_got.at[source], (me, source)).wait_recv()
    total = from_z[0]
    for s in range(1, depth_z):
        total = total + from_z[s]
    total = total * (1.0 / divisor)

    pieces = [total] + [pltpu.roll(total, LANES - KEEP * a, 1) for a in range(1, LANES // KEEP)]
    held = TILE * len(pieces)
    square = jnp.concatenate(pieces + [jnp.zeros((LANES - held, LANES), jnp.float32)], axis=0).T
    own = held // CORES
    square = jnp.where(core == 1, pltpu.roll(square, LANES - own, 1), square)
    taps = kernel_out.shape[0]
    kernel_out[...] = square[:taps, :own]
    norm_out[...] = square[taps : taps + 2, :own]

    for copy in core_copies + x_copies + z_copies:
        copy.wait_send()
    for away, copy in y_copies:
        pl.when(away)(copy.wait_send)
    stay.wait()
    move.wait()


def share_pass(grads, packed, taps):
    side = packed.shape[1]
    depth_z = lax.axis_size("group")
    share = side // CORES
    size, channels = grads.shape[1:]
    frames = CORES * size
    divisor = math.sqrt(lax.axis_size("dp") * depth_z * frames)
    own = channels // lax.axis_size("dp")
    vmem = pl.BlockSpec(memory_space=pltpu.VMEM)
    f32 = jnp.float32
    dma = pltpu.SemaphoreType.DMA
    return pl.pallas_call(
        lambda *refs: share_kernel(side, depth_z, divisor, *refs),
        out_shape=(
            jax.ShapeDtypeStruct((frames, channels), jnp.bfloat16),
            jax.ShapeDtypeStruct((taps, own), f32),
            jax.ShapeDtypeStruct((2, own), f32),
        ),
        in_specs=[vmem, vmem],
        out_specs=[pl.BlockSpec(memory_space=pl.ANY), vmem, vmem],
        scratch_shapes=[
            pltpu.VMEM((side, share, TILE, LANES), f32),
            pltpu.VMEM((side, share, TILE, LANES), f32),
            pltpu.VMEM((side - 1, share, TILE, LANES), f32),
            pltpu.VMEM((share, TILE, LANES), f32),
            pltpu.VMEM((side, TILE, LANES), f32),
            pltpu.VMEM((TILE, LANES), f32),
            pltpu.VMEM((depth_z, TILE, LANES), f32),
            dma((side,)), dma((side,)),
            dma((side - 1,)), dma((side - 1,)),
            dma((side,)), dma((side,)),
            dma((depth_z - 1,)), dma((depth_z,)),
            dma, dma, dma,
        ],
        compiler_params=pltpu.CompilerParams(collective_id=0, has_side_effects=True),
        name="share_terms",
    )(grads, packed)


def local(features, cotangent, lengths, destination, kernel, norm_gain, norm_bias):
    frames, channels = features.shape[2:]
    side = math.isqrt(lax.axis_size("dp") // CORES)
    grads, packed = local_pass(
        features[0, 0], cotangent[0, 0], lengths[0, 0], destination[0, 0], kernel, norm_gain, norm_bias, side
    )
    input_grad, kernel_grad, norm_grad = share_pass(grads, packed, kernel.shape[0])
    return (input_grad.reshape(1, 1, frames, channels), kernel_grad, norm_grad)


def solution(mesh):
    return jax.shard_map(
        local,
        mesh=mesh,
        in_specs=(
            P("dp", "group", None, None),
            P("dp", "group", None, None),
            P("dp", "group", None),
            P("dp", "group", None),
            P(),
            P(),
            P(),
        ),
        out_specs=(P("dp", "group", None, None), P(None, "dp"), P(None, "dp")),
        check_vma=False,
    )
```

```python
import math

import jax
import jax.numpy as jnp
from jax import lax
from jax.experimental import pallas as pl
from jax.experimental.pallas import tpu as pltpu
from jax.sharding import PartitionSpec as P

EPSILON = 1e-05
GAP = 16
LANES = 128
KEEP = 40
TILE = 8
CORES = 2
MOVES = 3
MESH = pl.DeviceIdType.MESH


def tap_groups(taps):
    return [[k for k in range(phase, taps, TILE)] for phase in range(TILE)]


def convolve(source, row, weights, taps, rows):
    total = None
    for group in tap_groups(taps):
        window = source[pl.ds(row + group[0], rows + TILE * (len(group) - 1)), :]
        for step, tap in enumerate(group):
            term = weights(tap) * window[TILE * step : TILE * step + rows]
            total = term if total is None else total + term
    return total


def block_kernel(
    side, depth_z, divisor,
    lengths, destination, features, cotangent, kernel, gain, bias,
    grad_out, tile_out,
    stage, padded, conv, dnorm, dconv, owner, row_a, row_b, mean, scale, tap_sums, terms, columnwise, packed, grads,
    from_core, sum_core, from_x, sum_x, from_y, sum_y, from_z,
    core_sent, core_got, x_sent, x_got, y_sent, y_got, z_sent, z_got, move_sent, move_got, stay_done,
):
    me = lax.axis_index("dp")
    z = lax.axis_index("group")
    ring = side * side * CORES
    core = lax.rem(me, CORES)
    chip = lax.div(me, CORES)
    y = lax.rem(chip, side)
    x = lax.div(chip, side)
    share = side // CORES

    def at(x, y, core):
        return ((x * side + y) * CORES + core, z)

    partner = at(x, y, 1 - core)
    following = (lax.rem(me + 1, ring), z)
    beside = (lax.rem(me + ring + 2 * core - 1, ring), z)
    x_steps = sorted(range(1, side), key=lambda d: -min(d, side - d))
    z_steps = sorted(range(1, depth_z), key=lambda d: -min(d, depth_z - d))

    def x_at(step):
        return lax.rem(x + step, side)

    def z_at(step):
        return lax.rem(z + step, depth_z)

    barrier = pltpu.get_barrier_semaphore()
    peers = [partner, beside]
    peers += [at(x_at(d), y, core) for d in range(1, side)]
    peers += [at(x, lax.rem(y + d, side), c) for d in range(1, side) for c in range(CORES)]
    peers += [(me, z_at(d)) for d in range(1, depth_z)]
    for peer in peers:
        pl.semaphore_signal(barrier, inc=1, device_id=peer, device_id_type=MESH)

    frames, channels = features.shape
    utterances = lengths.shape[0]
    taps = kernel.shape[0]
    half_span = taps // 2
    blocks = channels // LANES
    spread = frames + GAP * (utterances - 1)
    margin = GAP * (utterances - 1)
    chunk = spread // 2
    inverse = 1.0 / channels

    place = lax.broadcasted_iota(jnp.int32, (spread, LANES), 0)
    wide_owner = jnp.full((spread, LANES), -1, jnp.int32)
    begin = 0
    for u in range(utterances):
        finish = begin + lengths[u]
        here = (place >= begin + GAP * u) & (place < finish + GAP * u)
        wide_owner = jnp.where(here, u, wide_owner)
        begin = finish
    owner[...] = wide_owner

    edge = jnp.zeros((GAP, LANES), jnp.float32)
    terms[...] = jnp.zeros_like(terms)

    def spread_rows(value):
        stage[pl.ds(margin, frames), :] = value
        ids = owner[...]
        out = jnp.zeros((spread, LANES), jnp.float32)
        for u in range(utterances):
            out = jnp.where(ids == u, stage[pl.ds(margin - GAP * u, spread), :], out)
        return out

    def columns(b):
        return pl.ds(pl.multiple_of(b * LANES, LANES), LANES)

    def row_total(ref):
        return jnp.broadcast_to(jnp.sum(ref[...], axis=1, keepdims=True), (spread, LANES))

    stage[...] = jnp.zeros_like(stage)
    row_a[...] = jnp.zeros_like(row_a)

    @pl.loop(0, blocks)
    def _(b):
        padded[b, pl.ds(0, GAP), :] = edge
        padded[b, pl.ds(GAP + spread, GAP), :] = edge
        padded[b, pl.ds(GAP, spread), :] = spread_rows(features[:, columns(b)].astype(jnp.float32))
        for c in range(2):
            value = convolve(
                padded.at[b], GAP - half_span + chunk * c,
                lambda tap: kernel[pl.ds(tap, 1), columns(b)], taps, chunk,
            )
            conv[b, pl.ds(chunk * c, chunk), :] = value
            row_a[pl.ds(chunk * c, chunk), :] += value

    mean[...] = row_total(row_a) * inverse
    row_a[...] = jnp.zeros_like(row_a)

    @pl.loop(0, blocks)
    def _(b):
        centred = conv[b] - mean[...]
        conv[b] = centred
        row_a[...] += centred * centred

    scale[...] = lax.rsqrt(row_total(row_a) * inverse + EPSILON)
    row_a[...] = jnp.zeros_like(row_a)
    row_b[...] = jnp.zeros_like(row_b)

    @pl.loop(0, blocks)
    def _(b):
        normed = conv[b] * scale[...]
        conv[b] = normed
        g = gain[columns(b)][None]
        act = normed * g + bias[columns(b)][None]
        gate = jax.nn.sigmoid(act)
        dact = spread_rows(cotangent[:, columns(b)].astype(jnp.float32)) * gate * (1.0 + act * (1.0 - gate))
        terms[pl.ds(taps, 1), columns(b)] = jnp.sum(dact * normed, axis=0, keepdims=True)
        terms[pl.ds(taps + 1, 1), columns(b)] = jnp.sum(dact, axis=0, keepdims=True)
        weighted = dact * g
        dnorm[b] = weighted
        row_a[...] += weighted
        row_b[...] += weighted * normed

    mean[...] = row_total(row_a) * inverse
    row_b[...] = row_total(row_b) * inverse

    @pl.loop(0, blocks)
    def _(b):
        dconv[b, pl.ds(0, GAP), :] = edge
        dconv[b, pl.ds(GAP + spread, GAP), :] = edge
        dconv[b, pl.ds(GAP, spread), :] = scale[...] * (dnorm[b] - mean[...] - conv[b] * row_b[...])
        for c in range(2):
            ours = dconv[b, pl.ds(GAP + chunk * c, chunk), :]
            for group in tap_groups(taps):
                window = padded[
                    b, pl.ds(GAP - half_span + chunk * c + group[0], chunk + TILE * (len(group) - 1)), :
                ]
                for step, tap in enumerate(group):
                    product = ours * window[TILE * step : TILE * step + chunk]
                    part = jnp.sum(product.reshape(chunk // TILE, TILE, LANES), axis=0)
                    tap_sums[tap] = part if c == 0 else tap_sums[tap] + part
        terms[pl.ds(0, taps), columns(b)] = jnp.sum(tap_sums[...], axis=1)
        square = jnp.concatenate([terms[:, columns(b)], jnp.zeros((LANES - KEEP, LANES), jnp.float32)], axis=0)
        columnwise[columns(b), :] = square.T

    halves, lines, share = packed.shape[:3]
    depth = channels // (halves * lines * share)

    @pl.loop(0, lines)
    def _(x):
        for y in range(halves * share):
            first = (x * halves * share + y) * depth
            tile = None
            for a in range(depth // TILE):
                piece = columnwise[pl.ds(pl.multiple_of(first + TILE * a, TILE), TILE), :]
                piece = piece if a == 0 else pltpu.roll(piece, KEEP * a, 1)
                tile = piece if tile is None else tile + piece
            packed[y // share, x, y % share] = tile

    size = frames // destination.shape[0]

    def input_gradient(b):
        for c in range(2):
            stage[pl.ds(chunk * c, chunk), :] = convolve(
                dconv.at[b], GAP - half_span + chunk * c,
                lambda tap: kernel[pl.ds(taps - 1 - tap, 1), columns(b)], taps, chunk,
            )
        spot = lax.broadcasted_iota(jnp.int32, (frames, LANES), 0)
        grad = stage[pl.ds(0, frames), :]
        begin = lengths[0]
        for u in range(1, utterances):
            grad = jnp.where(spot >= begin, stage[pl.ds(GAP * u, frames), :], grad)
            begin = begin + lengths[u]
        top, bottom = grad[:size], grad[size:]
        keep_top = destination[0] == 0
        grads[0, :, columns(b)] = jnp.where(keep_top, top, bottom).astype(grads.dtype)
        grads[1, :, columns(b)] = jnp.where(keep_top, bottom, top).astype(grads.dtype)

    def remote(source, target, sent, got, device):
        return pltpu.make_async_remote_copy(
            src_ref=source, dst_ref=target, send_sem=sent, recv_sem=got, device_id=device, device_id_type=MESH
        )

    batch = blocks // MOVES
    moves = []

    def gradient_batch(i):
        pl.loop(batch * i, batch * (i + 1))(input_gradient)
        part = pl.ds(batch * LANES * i, batch * LANES)
        move = remote(
            grads.at[1, :, part], grad_out.at[pl.ds(size, size), part], move_sent.at[i], move_got.at[i], following
        )
        move.start()
        moves.append(move)

    pl.semaphore_wait(barrier, len(peers))
    core_copies = []
    for d in x_steps + [0]:
        row = x_at(d)
        copy = remote(packed.at[1 - core, row], from_core.at[row], core_sent.at[row], core_got.at[row], partner)
        copy.start()
        core_copies.append(copy)
    gradient_batch(0)
    x_copies = []
    for d in x_steps:
        row = x_at(d)
        remote(packed.at[1 - core, row], from_core.at[row], core_sent.at[row], core_got.at[row], partner).wait_recv()
        sum_core[row] = packed[core, row] + from_core[row]
        copy = remote(sum_core.at[row], from_x.at[d - 1], x_sent.at[d - 1], x_got.at[d - 1], at(row, y, core))
        copy.start()
        x_copies.append(copy)
    for i in range(1, MOVES):
        gradient_batch(i)
    stay = pltpu.make_async_copy(grads.at[0], grad_out.at[pl.ds(0, size)], stay_done)
    stay.start()

    remote(packed.at[1 - core, x], from_core.at[x], core_sent.at[x], core_got.at[x], partner).wait_recv()
    total = packed[core, x] + from_core[x]
    for d in reversed(x_steps):
        remote(sum_core.at[x], from_x.at[d - 1], x_sent.at[d - 1], x_got.at[d - 1], at(x, y, core)).wait_recv()
        total = total + from_x[d - 1]
    sum_x[...] = total

    holder = lax.div(y, share)
    y_copies = []
    for j in range(share):
        for c in range(CORES):
            goal = share * core + j
            away = jnp.logical_or(goal != y, core != c)
            copy = remote(
                sum_x.at[j], from_y.at[y], y_sent.at[j * CORES + c], y_got.at[y], at(x, goal, c)
            )
            pl.when(away)(copy.start)
            y_copies.append((away, copy))

    @pl.when(holder == core)
    def _():
        from_y[y] = sum_x[lax.rem(y, share)]

    for s in range(side):
        arrives = jnp.logical_or(s != y, holder != core)
        waiter = remote(sum_x.at[0], from_y.at[s], y_sent.at[0], y_got.at[s], at(x, s, holder))
        pl.when(arrives)(waiter.wait_recv)
    total = from_y[0]
    for s in range(1, side):
        total = total + from_y[s]
    sum_y[...] = total
    z_copies = []
    for d in z_steps:
        copy = remote(sum_y, from_z.at[z], z_sent.at[d - 1], z_got.at[z], (me, z_at(d)))
        copy.start()
        z_copies.append(copy)
    from_z[z] = total
    for d in z_steps:
        source = z_at(d)
        remote(sum_y, from_z.at[source], z_sent.at[d - 1], z_got.at[source], (me, source)).wait_recv()
    total = from_z[0]
    for s in range(1, depth_z):
        total = total + from_z[s]
    tile_out[...] = total * (1.0 / divisor)

    for copy in core_copies + x_copies + z_copies:
        copy.wait_send()
    for away, copy in y_copies:
        pl.when(away)(copy.wait_send)
    stay.wait()
    for move in moves:
        move.wait()


def block_pass(features, cotangent, lengths, destination, kernel, gain, bias):
    frames, channels = features.shape
    utterances = lengths.shape[0]
    taps = kernel.shape[0]
    size = frames // destination.shape[0]
    blocks = channels // LANES
    spread = frames + GAP * (utterances - 1)
    margin = GAP * (utterances - 1)
    side = math.isqrt(lax.axis_size("dp") // CORES)
    share = side // CORES
    depth_z = lax.axis_size("group")
    divisor = math.sqrt(lax.axis_size("dp") * depth_z * frames)
    smem = pl.BlockSpec(memory_space=pltpu.SMEM)
    vmem = pl.BlockSpec(memory_space=pltpu.VMEM)
    f32 = jnp.float32
    dma = pltpu.SemaphoreType.DMA
    return pl.pallas_call(
        lambda *refs: block_kernel(side, depth_z, divisor, *refs),
        out_shape=(
            jax.ShapeDtypeStruct((frames, channels), jnp.bfloat16),
            jax.ShapeDtypeStruct((TILE, LANES), f32),
        ),
        in_specs=[smem, smem] + [vmem] * 5,
        out_specs=[pl.BlockSpec(memory_space=pl.ANY), vmem],
        scratch_shapes=[
            pltpu.VMEM((margin + spread, LANES), f32),
            pltpu.VMEM((blocks, spread + 2 * GAP, LANES), f32),
            pltpu.VMEM((blocks, spread, LANES), f32),
            pltpu.VMEM((blocks, spread, LANES), f32),
            pltpu.VMEM((blocks, spread + 2 * GAP, LANES), f32),
            pltpu.VMEM((spread, LANES), jnp.int32),
            pltpu.VMEM((spread, LANES), f32),
            pltpu.VMEM((spread, LANES), f32),
            pltpu.VMEM((spread, LANES), f32),
            pltpu.VMEM((spread, LANES), f32),
            pltpu.VMEM((taps, TILE, LANES), f32),
            pltpu.VMEM((KEEP, channels), f32),
            pltpu.VMEM((channels, LANES), f32),
            pltpu.VMEM((CORES, side, share, TILE, LANES), f32),
            pltpu.VMEM((2, size, channels), jnp.bfloat16),
            pltpu.VMEM((side, share, TILE, LANES), f32),
            pltpu.VMEM((side, share, TILE, LANES), f32),
            pltpu.VMEM((side - 1, share, TILE, LANES), f32),
            pltpu.VMEM((share, TILE, LANES), f32),
            pltpu.VMEM((side, TILE, LANES), f32),
            pltpu.VMEM((TILE, LANES), f32),
            pltpu.VMEM((depth_z, TILE, LANES), f32),
            dma((side,)), dma((side,)),
            dma((side - 1,)), dma((side - 1,)),
            dma((side,)), dma((side,)),
            dma((depth_z - 1,)), dma((depth_z,)),
            dma((MOVES,)), dma((MOVES,)), dma,
        ],
        compiler_params=pltpu.CompilerParams(collective_id=0, has_side_effects=True),
        name="conv_block",
    )(lengths, destination, features, cotangent, kernel, gain, bias)


def finish_kernel(grads, tile, grad_out, kernel_out, norm_out, done):
    copy = pltpu.make_async_copy(grads, grad_out, done)
    copy.start()
    core = lax.rem(lax.axis_index("dp"), CORES)
    total = tile[...]
    pieces = [total] + [pltpu.roll(total, LANES - KEEP * a, 1) for a in range(1, LANES // KEEP)]
    square = jnp.concatenate(pieces, axis=0)
    own, taps = kernel_out.shape
    square = jnp.where(core == 1, square[own:], square[:own])
    kernel_out[...] = square[:, :taps]
    norm_out[...] = square[:, taps : taps + 2].T
    copy.wait()


def finish_pass(grads, tile, taps):
    own = grads.shape[1] // lax.axis_size("dp")
    vmem = pl.BlockSpec(memory_space=pltpu.VMEM)
    return pl.pallas_call(
        finish_kernel,
        out_shape=(
            jax.ShapeDtypeStruct(grads.shape, grads.dtype),
            jax.ShapeDtypeStruct((own, taps), jnp.float32),
            jax.ShapeDtypeStruct((2, own), jnp.float32),
        ),
        in_specs=[vmem, vmem],
        out_specs=[pl.BlockSpec(memory_space=pl.ANY), vmem, vmem],
        scratch_shapes=[pltpu.SemaphoreType.DMA],
        name="finish",
    )(grads, tile)


def local(features, cotangent, lengths, destination, kernel, norm_gain, norm_bias):
    grads, tile = block_pass(
        features[0, 0], cotangent[0, 0], lengths[0, 0], destination[0, 0], kernel, norm_gain, norm_bias
    )
    input_grad, kernel_grad, norm_grad = finish_pass(grads, tile, kernel.shape[0])
    return (input_grad.reshape(features.shape), kernel_grad.T, norm_grad)


def solution(mesh):
    return jax.shard_map(
        local,
        mesh=mesh,
        in_specs=(
            P("dp", "group", None, None),
            P("dp", "group", None, None),
            P("dp", "group", None),
            P("dp", "group", None),
            P(),
            P(),
            P(),
        ),
        out_specs=(P("dp", "group", None, None), P(None, "dp"), P(None, "dp")),
        check_vma=False,
    )
```

```python
import math

import jax
import jax.numpy as jnp
from jax import lax
from jax.experimental import pallas as pl
from jax.experimental.pallas import tpu as pltpu
from jax.sharding import PartitionSpec as P

EPSILON = 1e-05
GAP = 16
LANES = 128
KEEP = 40
TILE = 8
CORES = 2
MOVES = 4
PAIR = 2
MESH = pl.DeviceIdType.MESH


def tap_groups(taps):
    return [[k for k in range(phase, taps, TILE)] for phase in range(TILE)]


def convolve(source, row, weights, taps, rows):
    total = None
    for group in tap_groups(taps):
        window = source[pl.ds(row + group[0], rows + TILE * (len(group) - 1)), :]
        for step, tap in enumerate(group):
            term = weights(tap) * window[TILE * step : TILE * step + rows]
            total = term if total is None else total + term
    return total


def block_kernel(
    side, depth_z, divisor,
    lengths, destination, features, cotangent, kernel, gain, bias,
    grad_out, tile_out,
    stage, padded, conv, dnorm, dconv, owner, row_a, row_b, mean, scale, tap_sums, terms, columnwise, packed, grads,
    from_core, sum_core, from_x, sum_x, from_y, sum_y, from_z,
    core_sent, core_got, x_sent, x_got, y_sent, y_got, z_sent, z_got, move_sent, move_got, stay_done,
):
    me = lax.axis_index("dp")
    z = lax.axis_index("group")
    ring = side * side * CORES
    core = lax.rem(me, CORES)
    chip = lax.div(me, CORES)
    y = lax.rem(chip, side)
    x = lax.div(chip, side)
    share = side // CORES

    def at(x, y, core):
        return ((x * side + y) * CORES + core, z)

    partner = at(x, y, 1 - core)
    following = (lax.rem(me + 1, ring), z)
    beside = (lax.rem(me + ring + 2 * core - 1, ring), z)
    x_steps = sorted(range(1, side), key=lambda d: -min(d, side - d))
    z_steps = sorted(range(1, depth_z), key=lambda d: -min(d, depth_z - d))

    def x_at(step):
        return lax.rem(x + step, side)

    def z_at(step):
        return lax.rem(z + step, depth_z)

    barrier = pltpu.get_barrier_semaphore()
    peers = [partner, beside]
    peers += [at(x_at(d), y, core) for d in range(1, side)]
    peers += [at(x, lax.rem(y + d, side), c) for d in range(1, side) for c in range(CORES)]
    peers += [(me, z_at(d)) for d in range(1, depth_z)]
    for peer in peers:
        pl.semaphore_signal(barrier, inc=1, device_id=peer, device_id_type=MESH)

    frames, channels = features.shape
    utterances = lengths.shape[0]
    taps = kernel.shape[0]
    half_span = taps // 2
    blocks = channels // LANES
    spread = frames + GAP * (utterances - 1)
    margin = GAP * (utterances - 1)
    chunk = spread // 2
    inverse = 1.0 / channels

    place = lax.broadcasted_iota(jnp.int32, (spread, LANES), 0)
    wide_owner = jnp.full((spread, LANES), -1, jnp.int32)
    begin = 0
    for u in range(utterances):
        finish = begin + lengths[u]
        here = (place >= begin + GAP * u) & (place < finish + GAP * u)
        wide_owner = jnp.where(here, u, wide_owner)
        begin = finish
    owner[...] = wide_owner.astype(jnp.float32).astype(jnp.bfloat16)

    edge = jnp.zeros((GAP, LANES), jnp.float32)
    terms[...] = jnp.zeros_like(terms)

    def spread_rows(value):
        ids = owner[...]
        out = jnp.zeros((spread, LANES), value.dtype)
        for u in range(utterances):
            parts = [value]
            if u > 0:
                parts = [jnp.zeros((GAP * u, LANES), value.dtype)] + parts
            if u < utterances - 1:
                parts = parts + [jnp.zeros((margin - GAP * u, LANES), value.dtype)]
            out = jnp.where(ids == u, jnp.concatenate(parts, axis=0), out)
        return out.astype(jnp.float32)

    def columns(b):
        return pl.ds(pl.multiple_of(b * LANES, LANES), LANES)

    def row_total(ref):
        return jnp.broadcast_to(jnp.sum(ref[...], axis=1, keepdims=True), (spread, LANES))

    row_a[...] = jnp.zeros_like(row_a)

    @pl.loop(0, blocks)
    def _(b):
        padded[b, pl.ds(0, GAP), :] = edge
        padded[b, pl.ds(GAP + spread, GAP), :] = edge
        padded[b, pl.ds(GAP, spread), :] = spread_rows(features[:, columns(b)])
        for c in range(2):
            value = convolve(
                padded.at[b], GAP - half_span + chunk * c,
                lambda tap: kernel[pl.ds(tap, 1), columns(b)], taps, chunk,
            )
            conv[b, pl.ds(chunk * c, chunk), :] = value
            row_a[pl.ds(chunk * c, chunk), :] += value

    mean[...] = row_total(row_a) * inverse
    row_a[...] = jnp.zeros_like(row_a)

    @pl.loop(0, blocks)
    def _(b):
        centred = conv[b] - mean[...]
        conv[b] = centred
        row_a[...] += centred * centred

    scale[...] = lax.rsqrt(row_total(row_a) * inverse + EPSILON)
    row_a[...] = jnp.zeros_like(row_a)
    row_b[...] = jnp.zeros_like(row_b)

    @pl.loop(0, blocks)
    def _(b):
        normed = conv[b] * scale[...]
        conv[b] = normed
        g = gain[columns(b)][None]
        act = normed * g + bias[columns(b)][None]
        gate = 0.5 * jnp.tanh(0.5 * act) + 0.5
        dact = spread_rows(cotangent[:, columns(b)]) * gate * (1.0 + act * (1.0 - gate))
        terms[pl.ds(taps, 1), columns(b)] = jnp.sum(dact * normed, axis=0, keepdims=True)
        terms[pl.ds(taps + 1, 1), columns(b)] = jnp.sum(dact, axis=0, keepdims=True)
        weighted = dact * g
        dnorm[b] = weighted
        row_a[...] += weighted
        row_b[...] += weighted * normed

    mean[...] = row_total(row_a) * inverse
    row_b[...] = row_total(row_b) * inverse

    def kernel_terms(b):
        dconv[b, pl.ds(0, GAP), :] = edge
        dconv[b, pl.ds(GAP + spread, GAP), :] = edge
        dconv[b, pl.ds(GAP, spread), :] = scale[...] * (dnorm[b] - mean[...] - conv[b] * row_b[...])
        for c in range(2):
            ours = dconv[b, pl.ds(GAP + chunk * c, chunk), :]
            for group in tap_groups(taps):
                window = padded[
                    b, pl.ds(GAP - half_span + chunk * c + group[0], chunk + TILE * (len(group) - 1)), :
                ]
                for step, tap in enumerate(group):
                    product = ours * window[TILE * step : TILE * step + chunk]
                    part = jnp.sum(product.reshape(chunk // TILE, TILE, LANES), axis=0)
                    tap_sums[tap] = part if c == 0 else tap_sums[tap] + part
        terms[pl.ds(0, taps), columns(b)] = jnp.sum(tap_sums[...], axis=1)
        square = jnp.concatenate([terms[:, columns(b)], jnp.zeros((LANES - KEEP, LANES), jnp.float32)], axis=0)
        columnwise[columns(b), :] = square.T

    depth = channels // (side * side)

    def pack_row(row):
        for column in range(side):
            first = (row * side + column) * depth
            tile = None
            for a in range(depth // TILE):
                piece = columnwise[pl.ds(pl.multiple_of(first + TILE * a, TILE), TILE), :]
                piece = piece if a == 0 else pltpu.roll(piece, KEEP * a, 1)
                tile = piece if tile is None else tile + piece
            packed[column // share, row, column % share] = tile

    def remote(source, target, sent, got, device):
        return pltpu.make_async_remote_copy(
            src_ref=source, dst_ref=target, send_sem=sent, recv_sem=got, device_id=device, device_id_type=MESH
        )

    def core_copy(row):
        return remote(packed.at[1 - core, row], from_core.at[row], core_sent.at[row], core_got.at[row], partner)

    def x_copy(row, d):
        return remote(sum_core.at[row], from_x.at[d], x_sent.at[d], x_got.at[d], at(row, y, core))

    def forward(pair):
        for r in range(PAIR):
            row = pair * PAIR + r
            core_copy(row).wait_recv()
            sum_core[row] = packed[core, row] + from_core[row]
            d = lax.rem(row - x + side, side)
            pl.when(d != 0)(x_copy(row, d).start)

    pl.semaphore_wait(barrier, len(peers))
    groups = side // PAIR
    width = blocks // groups
    own_pair = lax.div(x, PAIR)

    @pl.loop(0, groups)
    def _(i):
        pair = lax.rem(own_pair + 1 + i, groups)
        pl.loop(0, width)(lambda t: kernel_terms(pair * width + t))
        for r in range(PAIR):
            pack_row(pair * PAIR + r)
            core_copy(pair * PAIR + r).start()
        pl.when(i > 0)(lambda: forward(lax.rem(pair + groups - 1, groups)))

    size = frames // destination.shape[0]

    def input_gradient(b):
        for c in range(2):
            stage[pl.ds(chunk * c, chunk), :] = convolve(
                dconv.at[b], GAP - half_span + chunk * c,
                lambda tap: kernel[pl.ds(taps - 1 - tap, 1), columns(b)], taps, chunk,
            )
        spot = lax.broadcasted_iota(jnp.int32, (frames, LANES), 0)
        grad = stage[pl.ds(0, frames), :]
        begin = lengths[0]
        for u in range(1, utterances):
            grad = jnp.where(spot >= begin, stage[pl.ds(GAP * u, frames), :], grad)
            begin = begin + lengths[u]
        top, bottom = grad[:size], grad[size:]
        keep_top = destination[0] == 0
        grads[0, :, columns(b)] = jnp.where(keep_top, top, bottom).astype(grads.dtype)
        grads[1, :, columns(b)] = jnp.where(keep_top, bottom, top).astype(grads.dtype)

    batch = blocks // MOVES
    moves = []

    def gradient_batch(i):
        pl.loop(batch * i, batch * (i + 1))(input_gradient)
        part = pl.ds(batch * LANES * i, batch * LANES)
        move = remote(
            grads.at[1, :, part], grad_out.at[pl.ds(size, size), part], move_sent.at[i], move_got.at[i], following
        )
        move.start()
        moves.append(move)

    gradient_batch(0)
    forward(own_pair)
    gradient_batch(1)
    total = sum_core[x]
    for d in reversed(x_steps):
        x_copy(x, d).wait_recv()
        total = total + from_x[d]
    sum_x[...] = total

    holder = lax.div(y, share)
    y_copies = []
    for j in range(share):
        for c in range(CORES):
            goal = share * core + j
            away = jnp.logical_or(goal != y, core != c)
            copy = remote(
                sum_x.at[j], from_y.at[y], y_sent.at[j * CORES + c], y_got.at[y], at(x, goal, c)
            )
            pl.when(away)(copy.start)
            y_copies.append((away, copy))

    @pl.when(holder == core)
    def _():
        from_y[y] = sum_x[lax.rem(y, share)]

    for i in range(2, MOVES):
        gradient_batch(i)
    stay = pltpu.make_async_copy(grads.at[0], grad_out.at[pl.ds(0, size)], stay_done)
    stay.start()

    for s in range(side):
        arrives = jnp.logical_or(s != y, holder != core)
        waiter = remote(sum_x.at[0], from_y.at[s], y_sent.at[0], y_got.at[s], at(x, s, holder))
        pl.when(arrives)(waiter.wait_recv)
    total = from_y[0]
    for s in range(1, side):
        total = total + from_y[s]
    sum_y[...] = total
    z_copies = []
    for d in z_steps:
        copy = remote(sum_y, from_z.at[z], z_sent.at[d - 1], z_got.at[z], (me, z_at(d)))
        copy.start()
        z_copies.append(copy)
    from_z[z] = total
    for d in z_steps:
        source = z_at(d)
        remote(sum_y, from_z.at[source], z_sent.at[d - 1], z_got.at[source], (me, source)).wait_recv()
    total = from_z[0]
    for s in range(1, depth_z):
        total = total + from_z[s]
    tile_out[...] = total * (1.0 / divisor)

    for row in range(side):
        core_copy(row).wait_send()
    for d in x_steps:
        x_copy(x_at(d), d).wait_send()
    for copy in z_copies:
        copy.wait_send()
    for away, copy in y_copies:
        pl.when(away)(copy.wait_send)
    stay.wait()
    for move in moves:
        move.wait()


def block_pass(features, cotangent, lengths, destination, kernel, gain, bias):
    frames, channels = features.shape
    utterances = lengths.shape[0]
    taps = kernel.shape[0]
    size = frames // destination.shape[0]
    blocks = channels // LANES
    spread = frames + GAP * (utterances - 1)
    margin = GAP * (utterances - 1)
    side = math.isqrt(lax.axis_size("dp") // CORES)
    share = side // CORES
    depth_z = lax.axis_size("group")
    divisor = math.sqrt(lax.axis_size("dp") * depth_z * frames)
    smem = pl.BlockSpec(memory_space=pltpu.SMEM)
    vmem = pl.BlockSpec(memory_space=pltpu.VMEM)
    f32 = jnp.float32
    dma = pltpu.SemaphoreType.DMA
    return pl.pallas_call(
        lambda *refs: block_kernel(side, depth_z, divisor, *refs),
        out_shape=(
            pltpu.VMEM((frames, channels), jnp.bfloat16),
            pltpu.VMEM((TILE, LANES), f32),
        ),
        in_specs=[smem, smem] + [vmem] * 5,
        out_specs=[vmem, vmem],
        scratch_shapes=[
            pltpu.VMEM((margin + spread, LANES), f32),
            pltpu.VMEM((blocks, spread + 2 * GAP, LANES), f32),
            pltpu.VMEM((blocks, spread, LANES), f32),
            pltpu.VMEM((blocks, spread, LANES), f32),
            pltpu.VMEM((blocks, spread + 2 * GAP, LANES), f32),
            pltpu.VMEM((spread, LANES), jnp.bfloat16),
            pltpu.VMEM((spread, LANES), f32),
            pltpu.VMEM((spread, LANES), f32),
            pltpu.VMEM((spread, LANES), f32),
            pltpu.VMEM((spread, LANES), f32),
            pltpu.VMEM((taps, TILE, LANES), f32),
            pltpu.VMEM((KEEP, channels), f32),
            pltpu.VMEM((channels, LANES), f32),
            pltpu.VMEM((CORES, side, share, TILE, LANES), f32),
            pltpu.VMEM((2, size, channels), jnp.bfloat16),
            pltpu.VMEM((side, share, TILE, LANES), f32),
            pltpu.VMEM((side, share, TILE, LANES), f32),
            pltpu.VMEM((side, share, TILE, LANES), f32),
            pltpu.VMEM((share, TILE, LANES), f32),
            pltpu.VMEM((side, TILE, LANES), f32),
            pltpu.VMEM((TILE, LANES), f32),
            pltpu.VMEM((depth_z, TILE, LANES), f32),
            dma((side,)), dma((side,)),
            dma((side,)), dma((side,)),
            dma((side,)), dma((side,)),
            dma((depth_z - 1,)), dma((depth_z,)),
            dma((MOVES,)), dma((MOVES,)), dma,
        ],
        compiler_params=pltpu.CompilerParams(collective_id=0, has_side_effects=True),
        name="conv_block",
    )(lengths, destination, features, cotangent, kernel, gain, bias)


def finish_kernel(grads, tile, grad_out, kernel_out, norm_out, done):
    copy = pltpu.make_async_copy(grads, grad_out, done)
    copy.start()
    core = lax.rem(lax.axis_index("dp"), CORES)
    total = tile[...]
    pieces = [total] + [pltpu.roll(total, LANES - KEEP * a, 1) for a in range(1, LANES // KEEP)]
    square = jnp.concatenate(pieces, axis=0)
    own, taps = kernel_out.shape
    square = jnp.where(core == 1, square[own:], square[:own])
    kernel_out[...] = square[:, :taps]
    norm_out[...] = square[:, taps : taps + 2].T
    copy.wait()


def finish_pass(grads, tile, taps):
    own = grads.shape[1] // lax.axis_size("dp")
    vmem = pl.BlockSpec(memory_space=pltpu.VMEM)
    return pl.pallas_call(
        finish_kernel,
        out_shape=(
            jax.ShapeDtypeStruct(grads.shape, grads.dtype),
            jax.ShapeDtypeStruct((own, taps), jnp.float32),
            jax.ShapeDtypeStruct((2, own), jnp.float32),
        ),
        in_specs=[vmem, vmem],
        out_specs=[pl.BlockSpec(memory_space=pl.ANY), vmem, vmem],
        scratch_shapes=[pltpu.SemaphoreType.DMA],
        name="finish",
    )(pltpu.with_memory_space_constraint(grads, pltpu.VMEM), pltpu.with_memory_space_constraint(tile, pltpu.VMEM))


def local(features, cotangent, lengths, destination, kernel, norm_gain, norm_bias):
    grads, tile = block_pass(
        features[0, 0], cotangent[0, 0], lengths[0, 0], destination[0, 0], kernel, norm_gain, norm_bias
    )
    input_grad, kernel_grad, norm_grad = finish_pass(grads, tile, kernel.shape[0])
    return (input_grad.reshape(features.shape), kernel_grad.T, norm_grad)


def solution(mesh):
    return jax.shard_map(
        local,
        mesh=mesh,
        in_specs=(
            P("dp", "group", None, None),
            P("dp", "group", None, None),
            P("dp", "group", None),
            P("dp", "group", None),
            P(),
            P(),
            P(),
        ),
        out_specs=(P("dp", "group", None, None), P(None, "dp"), P(None, "dp")),
        check_vma=False,
    )
```

```python
import math

import jax
import jax.numpy as jnp
from jax import lax
from jax.experimental import pallas as pl
from jax.experimental.pallas import tpu as pltpu
from jax.sharding import PartitionSpec as P

EPSILON = 1e-05
GAP = 16
LANES = 128
KEEP = 40
TILE = 8
CORES = 2
MOVES = 4
PAIR = 2
PARTS = 3
MESH = pl.DeviceIdType.MESH


def tap_groups(taps):
    return [[k for k in range(phase, taps, TILE)] for phase in range(TILE)]


def convolve(source, row, weights, taps, rows):
    total = None
    for group in tap_groups(taps):
        window = source[pl.ds(row + group[0], rows + TILE * (len(group) - 1)), :]
        for step, tap in enumerate(group):
            term = weights(tap) * window[TILE * step : TILE * step + rows]
            total = term if total is None else total + term
    return total


def block_kernel(
    side, depth_z, divisor,
    lengths, destination, features, cotangent, kernel, gain, bias,
    grad_out, tile_out,
    stage, padded, conv, dnorm, dconv, spreading, row_a, row_b, mean, scale, tap_sums, terms, columnwise, packed, grads,
    from_core, sum_core, from_x, sum_x, from_y, sum_y, from_z,
    core_sent, core_got, x_sent, x_got, y_sent, y_got, z_sent, z_got, move_sent, move_got, stay_done,
):
    me = lax.axis_index("dp")
    z = lax.axis_index("group")
    ring = side * side * CORES
    core = lax.rem(me, CORES)
    chip = lax.div(me, CORES)
    y = lax.rem(chip, side)
    x = lax.div(chip, side)
    share = side // CORES

    def at(x, y, core):
        return ((x * side + y) * CORES + core, z)

    partner = at(x, y, 1 - core)
    following = (lax.rem(me + 1, ring), z)
    beside = (lax.rem(me + ring + 2 * core - 1, ring), z)
    x_steps = sorted(range(1, side), key=lambda d: -min(d, side - d))
    z_steps = sorted(range(1, depth_z), key=lambda d: -min(d, depth_z - d))

    def x_at(step):
        return lax.rem(x + step, side)

    def z_at(step):
        return lax.rem(z + step, depth_z)

    barrier = pltpu.get_barrier_semaphore()
    peers = [partner, beside]
    peers += [at(x_at(d), y, core) for d in range(1, side)]
    peers += [at(x, lax.rem(y + d, side), c) for d in range(1, side) for c in range(CORES)]
    peers += [(me, z_at(d)) for d in range(1, depth_z)]
    for peer in peers:
        pl.semaphore_signal(barrier, inc=1, device_id=peer, device_id_type=MESH)

    frames, channels = features.shape
    utterances = lengths.shape[0]
    taps = kernel.shape[0]
    half_span = taps // 2
    blocks = channels // LANES
    spread = frames + GAP * (utterances - 1)
    tiles = spread // TILE
    marks = [TILE * ((tiles * c + PARTS - 1) // PARTS) for c in range(PARTS + 1)]
    spans = [(marks[c], marks[c + 1] - marks[c]) for c in range(PARTS)]
    inverse = 1.0 / channels

    frame = lax.broadcasted_iota(jnp.int32, (spread, frames), 1)
    place = lax.broadcasted_iota(jnp.int32, (spread, frames), 0)
    shift, finish = 0, 0
    for u in range(utterances - 1):
        finish = finish + lengths[u]
        shift = shift + jnp.where(frame >= finish, GAP, 0)
    spreading[...] = jnp.where(place == frame + shift, 1.0, 0.0).astype(jnp.bfloat16)

    edge = jnp.zeros((GAP, LANES), jnp.float32)
    terms[...] = jnp.zeros_like(terms)

    def columns(b):
        return pl.ds(pl.multiple_of(b * LANES, LANES), LANES)

    def row_total(ref):
        return jnp.broadcast_to(jnp.sum(ref[...], axis=1, keepdims=True), (spread, LANES))

    row_a[...] = jnp.zeros_like(row_a)

    @pl.loop(0, blocks // PAIR)
    def _(i):
        part = pl.ds(pl.multiple_of(i * PAIR * LANES, PAIR * LANES), PAIR * LANES)
        spread_features = jnp.dot(spreading[...], features[:, part], preferred_element_type=jnp.float32)
        spread_cotangent = jnp.dot(spreading[...], cotangent[:, part], preferred_element_type=jnp.float32)
        for r in range(PAIR):
            padded[PAIR * i + r, pl.ds(GAP, spread), :] = spread_features[:, LANES * r : LANES * (r + 1)]
            dnorm[PAIR * i + r] = spread_cotangent[:, LANES * r : LANES * (r + 1)]

    @pl.loop(0, blocks)
    def _(b):
        padded[b, pl.ds(0, GAP), :] = edge
        padded[b, pl.ds(GAP + spread, GAP), :] = edge
        for begin, chunk in spans:
            value = convolve(
                padded.at[b], GAP - half_span + begin,
                lambda tap: kernel[pl.ds(tap, 1), columns(b)], taps, chunk,
            )
            conv[b, pl.ds(begin, chunk), :] = value
            row_a[pl.ds(begin, chunk), :] += value

    mean[...] = row_total(row_a) * inverse
    row_a[...] = jnp.zeros_like(row_a)

    @pl.loop(0, blocks)
    def _(b):
        centred = conv[b] - mean[...]
        conv[b] = centred
        row_a[...] += centred * centred

    scale[...] = lax.rsqrt(row_total(row_a) * inverse + EPSILON)
    row_a[...] = jnp.zeros_like(row_a)
    row_b[...] = jnp.zeros_like(row_b)

    @pl.loop(0, blocks)
    def _(b):
        normed = conv[b] * scale[...]
        conv[b] = normed
        g = gain[columns(b)][None]
        act = normed * g + bias[columns(b)][None]
        gate = 0.5 * jnp.tanh(0.5 * act) + 0.5
        dact = dnorm[b] * gate * (1.0 + act * (1.0 - gate))
        terms[pl.ds(taps, 1), columns(b)] = jnp.sum(dact * normed, axis=0, keepdims=True)
        terms[pl.ds(taps + 1, 1), columns(b)] = jnp.sum(dact, axis=0, keepdims=True)
        weighted = dact * g
        dnorm[b] = weighted
        row_a[...] += weighted
        row_b[...] += weighted * normed

    mean[...] = row_total(row_a) * inverse
    row_b[...] = row_total(row_b) * inverse

    def kernel_terms(b):
        dconv[b, pl.ds(0, GAP), :] = edge
        dconv[b, pl.ds(GAP + spread, GAP), :] = edge
        dconv[b, pl.ds(GAP, spread), :] = scale[...] * (dnorm[b] - mean[...] - conv[b] * row_b[...])
        for begin, chunk in spans:
            ours = dconv[b, pl.ds(GAP + begin, chunk), :]
            for group in tap_groups(taps):
                window = padded[
                    b, pl.ds(GAP - half_span + begin + group[0], chunk + TILE * (len(group) - 1)), :
                ]
                for step, tap in enumerate(group):
                    product = ours * window[TILE * step : TILE * step + chunk]
                    part = jnp.sum(product.reshape(chunk // TILE, TILE, LANES), axis=0)
                    tap_sums[tap] = part if begin == 0 else tap_sums[tap] + part
        terms[pl.ds(0, taps), columns(b)] = jnp.sum(tap_sums[...], axis=1)
        square = jnp.concatenate([terms[:, columns(b)], jnp.zeros((LANES - KEEP, LANES), jnp.float32)], axis=0)
        columnwise[columns(b), :] = square.T

    depth = channels // (side * side)

    def pack_row(row):
        for column in range(side):
            first = (row * side + column) * depth
            tile = None
            for a in range(depth // TILE):
                piece = columnwise[pl.ds(pl.multiple_of(first + TILE * a, TILE), TILE), :]
                piece = piece if a == 0 else pltpu.roll(piece, KEEP * a, 1)
                tile = piece if tile is None else tile + piece
            packed[column // share, row, column % share] = tile

    def remote(source, target, sent, got, device):
        return pltpu.make_async_remote_copy(
            src_ref=source, dst_ref=target, send_sem=sent, recv_sem=got, device_id=device, device_id_type=MESH
        )

    def core_copy(row):
        return remote(packed.at[1 - core, row], from_core.at[row], core_sent.at[row], core_got.at[row], partner)

    def x_copy(row, d):
        return remote(sum_core.at[row], from_x.at[d], x_sent.at[d], x_got.at[d], at(row, y, core))

    def forward(pair):
        for r in range(PAIR):
            row = pair * PAIR + r
            core_copy(row).wait_recv()
            sum_core[row] = packed[core, row] + from_core[row]
            d = lax.rem(row - x + side, side)
            pl.when(d != 0)(x_copy(row, d).start)

    pl.semaphore_wait(barrier, len(peers))
    groups = side // PAIR
    width = blocks // groups
    own_pair = lax.div(x, PAIR)

    @pl.loop(0, groups)
    def _(i):
        pair = lax.rem(own_pair + 1 + i, groups)
        pl.loop(0, width)(lambda t: kernel_terms(pair * width + t))
        for r in range(PAIR):
            pack_row(pair * PAIR + r)
            core_copy(pair * PAIR + r).start()
        pl.when(i > 0)(lambda: forward(lax.rem(pair + groups - 1, groups)))

    size = frames // destination.shape[0]

    def input_gradient(b):
        for begin, chunk in spans:
            stage[pl.ds(begin, chunk), :] = convolve(
                dconv.at[b], GAP - half_span + begin,
                lambda tap: kernel[pl.ds(taps - 1 - tap, 1), columns(b)], taps, chunk,
            )
        spot = lax.broadcasted_iota(jnp.int32, (frames, LANES), 0)
        grad = stage[pl.ds(0, frames), :]
        begin = lengths[0]
        for u in range(1, utterances):
            grad = jnp.where(spot >= begin, stage[pl.ds(GAP * u, frames), :], grad)
            begin = begin + lengths[u]
        top, bottom = grad[:size], grad[size:]
        keep_top = destination[0] == 0
        grads[0, :, columns(b)] = jnp.where(keep_top, top, bottom).astype(grads.dtype)
        grads[1, :, columns(b)] = jnp.where(keep_top, bottom, top).astype(grads.dtype)

    batch = blocks // MOVES
    moves = []

    def gradient_batch(i):
        pl.loop(batch * i, batch * (i + 1))(input_gradient)
        part = pl.ds(batch * LANES * i, batch * LANES)
        move = remote(
            grads.at[1, :, part], grad_out.at[pl.ds(size, size), part], move_sent.at[i], move_got.at[i], following
        )
        move.start()
        moves.append(move)

    gradient_batch(0)
    forward(own_pair)
    gradient_batch(1)
    total = sum_core[x]
    for d in reversed(x_steps):
        x_copy(x, d).wait_recv()
        total = total + from_x[d]
    sum_x[...] = total

    holder = lax.div(y, share)
    y_copies = []
    for j in range(share):
        for c in range(CORES):
            goal = share * core + j
            away = jnp.logical_or(goal != y, core != c)
            copy = remote(
                sum_x.at[j], from_y.at[y], y_sent.at[j * CORES + c], y_got.at[y], at(x, goal, c)
            )
            pl.when(away)(copy.start)
            y_copies.append((away, copy))

    @pl.when(holder == core)
    def _():
        from_y[y] = sum_x[lax.rem(y, share)]

    for i in range(2, MOVES):
        gradient_batch(i)
    stay = pltpu.make_async_copy(grads.at[0], grad_out.at[pl.ds(0, size)], stay_done)
    stay.start()

    for s in range(side):
        arrives = jnp.logical_or(s != y, holder != core)
        waiter = remote(sum_x.at[0], from_y.at[s], y_sent.at[0], y_got.at[s], at(x, s, holder))
        pl.when(arrives)(waiter.wait_recv)
    total = from_y[0]
    for s in range(1, side):
        total = total + from_y[s]
    sum_y[...] = total
    z_copies = []
    for d in z_steps:
        copy = remote(sum_y, from_z.at[z], z_sent.at[d - 1], z_got.at[z], (me, z_at(d)))
        copy.start()
        z_copies.append(copy)
    from_z[z] = total
    for d in z_steps:
        source = z_at(d)
        remote(sum_y, from_z.at[source], z_sent.at[d - 1], z_got.at[source], (me, source)).wait_recv()
    total = from_z[0]
    for s in range(1, depth_z):
        total = total + from_z[s]
    tile_out[...] = total * (1.0 / divisor)

    for row in range(side):
        core_copy(row).wait_send()
    for d in x_steps:
        x_copy(x_at(d), d).wait_send()
    for copy in z_copies:
        copy.wait_send()
    for away, copy in y_copies:
        pl.when(away)(copy.wait_send)
    stay.wait()
    for move in moves:
        move.wait()


def block_pass(features, cotangent, lengths, destination, kernel, gain, bias):
    frames, channels = features.shape
    utterances = lengths.shape[0]
    taps = kernel.shape[0]
    size = frames // destination.shape[0]
    blocks = channels // LANES
    spread = frames + GAP * (utterances - 1)
    margin = GAP * (utterances - 1)
    side = math.isqrt(lax.axis_size("dp") // CORES)
    share = side // CORES
    depth_z = lax.axis_size("group")
    divisor = math.sqrt(lax.axis_size("dp") * depth_z * frames)
    smem = pl.BlockSpec(memory_space=pltpu.SMEM)
    vmem = pl.BlockSpec(memory_space=pltpu.VMEM)
    f32 = jnp.float32
    dma = pltpu.SemaphoreType.DMA
    return pl.pallas_call(
        lambda *refs: block_kernel(side, depth_z, divisor, *refs),
        out_shape=(
            pltpu.VMEM((frames, channels), jnp.bfloat16),
            pltpu.VMEM((TILE, LANES), f32),
        ),
        in_specs=[smem, smem] + [vmem] * 5,
        out_specs=[vmem, vmem],
        scratch_shapes=[
            pltpu.VMEM((margin + spread, LANES), f32),
            pltpu.VMEM((blocks, spread + 2 * GAP, LANES), f32),
            pltpu.VMEM((blocks, spread, LANES), f32),
            pltpu.VMEM((blocks, spread, LANES), f32),
            pltpu.VMEM((blocks, spread + 2 * GAP, LANES), f32),
            pltpu.VMEM((spread, frames), jnp.bfloat16),
            pltpu.VMEM((spread, LANES), f32),
            pltpu.VMEM((spread, LANES), f32),
            pltpu.VMEM((spread, LANES), f32),
            pltpu.VMEM((spread, LANES), f32),
            pltpu.VMEM((taps, TILE, LANES), f32),
            pltpu.VMEM((KEEP, channels), f32),
            pltpu.VMEM((channels, LANES), f32),
            pltpu.VMEM((CORES, side, share, TILE, LANES), f32),
            pltpu.VMEM((2, size, channels), jnp.bfloat16),
            pltpu.VMEM((side, share, TILE, LANES), f32),
            pltpu.VMEM((side, share, TILE, LANES), f32),
            pltpu.VMEM((side, share, TILE, LANES), f32),
            pltpu.VMEM((share, TILE, LANES), f32),
            pltpu.VMEM((side, TILE, LANES), f32),
            pltpu.VMEM((TILE, LANES), f32),
            pltpu.VMEM((depth_z, TILE, LANES), f32),
            dma((side,)), dma((side,)),
            dma((side,)), dma((side,)),
            dma((side,)), dma((side,)),
            dma((depth_z - 1,)), dma((depth_z,)),
            dma((MOVES,)), dma((MOVES,)), dma,
        ],
        compiler_params=pltpu.CompilerParams(collective_id=0, has_side_effects=True),
        name="conv_block",
    )(lengths, destination, features, cotangent, kernel, gain, bias)


def finish_kernel(grads, tile, grad_out, kernel_out, norm_out, done):
    copy = pltpu.make_async_copy(grads, grad_out, done)
    copy.start()
    core = lax.rem(lax.axis_index("dp"), CORES)
    total = tile[...]
    pieces = [total] + [pltpu.roll(total, LANES - KEEP * a, 1) for a in range(1, LANES // KEEP)]
    square = jnp.concatenate(pieces, axis=0)
    own, taps = kernel_out.shape
    square = jnp.where(core == 1, square[own:], square[:own])
    kernel_out[...] = square[:, :taps]
    norm_out[...] = square[:, taps : taps + 2].T
    copy.wait()


def finish_pass(grads, tile, taps):
    own = grads.shape[1] // lax.axis_size("dp")
    vmem = pl.BlockSpec(memory_space=pltpu.VMEM)
    return pl.pallas_call(
        finish_kernel,
        out_shape=(
            jax.ShapeDtypeStruct(grads.shape, grads.dtype),
            jax.ShapeDtypeStruct((own, taps), jnp.float32),
            jax.ShapeDtypeStruct((2, own), jnp.float32),
        ),
        in_specs=[vmem, vmem],
        out_specs=[pl.BlockSpec(memory_space=pl.ANY), vmem, vmem],
        scratch_shapes=[pltpu.SemaphoreType.DMA],
        name="finish",
    )(pltpu.with_memory_space_constraint(grads, pltpu.VMEM), pltpu.with_memory_space_constraint(tile, pltpu.VMEM))


def local(features, cotangent, lengths, destination, kernel, norm_gain, norm_bias):
    grads, tile = block_pass(
        features[0, 0], cotangent[0, 0], lengths[0, 0], destination[0, 0], kernel, norm_gain, norm_bias
    )
    input_grad, kernel_grad, norm_grad = finish_pass(grads, tile, kernel.shape[0])
    return (input_grad.reshape(features.shape), kernel_grad.T, norm_grad)


def solution(mesh):
    return jax.shard_map(
        local,
        mesh=mesh,
        in_specs=(
            P("dp", "group", None, None),
            P("dp", "group", None, None),
            P("dp", "group", None),
            P("dp", "group", None),
            P(),
            P(),
            P(),
        ),
        out_specs=(P("dp", "group", None, None), P(None, "dp"), P(None, "dp")),
        check_vma=False,
    )
```
